32 devices in a mesh: row: 8 (over y, x, core), col: 4 (over z).
Axes of the slice: x: 2, y: 2, z: 4, core: 2. Of those that a mesh axis runs over, the one named last changes fastest.
Arguments:
- inputs_act: bfloat16 [1024, 4096], P('row', 'col'), may hold values from -6 to 6
- out_grad: bfloat16 [1024, 4096], P('row', 'col'), may hold values from -6 to 6
- pre_act: bfloat16 [1024, 16384], P('col', 'row'), may hold values from -8 to 8
- w_first: bfloat16 [4096, 16384], P('col', 'row'), may hold values from -0.046875 to 0.046875
- w_second: bfloat16 [16384, 4096], P('row', 'col'), may hold values from -0.09375 to 0.09375
Outputs:
- grad_input: bfloat16 [1024, 4096], P('row', 'col')
- grad_first: float32 [4096, 16384], P('col', 'row')
- grad_second: float32 [16384, 4096], P('row', 'col')
The draws below stay inside these ranges and needn't reach their ends.
All inputs are finite; a program needn't handle non-finite values.
Results may differ from the reference program's by a relative error of at most 0.019.
Values may be sent and summed in bfloat16 or wider, within the bound.
A program may use at most 128 MiB of HBM per device.

```python
import math
import jax
import jax.numpy as jnp
from jax import lax

D = 4096
H = 16384
TOKENS = 1024
N_ROW = 8


def shard_levels(key, extent, cuts, low, largest):
    def one(dim, blocks):
        draws = jax.random.uniform(jax.random.fold_in(jax.random.fold_in(key, 6), dim), (blocks,), jnp.float32, low / len(cuts), largest / len(cuts))
        return jnp.repeat(jnp.exp(draws), extent[dim] // blocks).reshape((-1,) + (1,) * (len(extent) - dim - 1))

    level = one(*cuts[0])
    for cut in cuts[1:]:
        level = level * one(*cut)
    return level


def normal_values(rng, shape, spread, bound, pieces=(), held_as=jnp.bfloat16):
    array = jax.random.normal(rng, shape, jnp.float32) * spread
    if len(pieces) > 0:
        array = shard_levels(rng, shape, pieces, -0.22, 0.18) * array
    return jnp.clip(array, min=-bound, max=bound).astype(held_as)


def setup_inputs(seed: int = 0) -> dict:
    key_of = jax.random.split(jax.random.key(seed), 6)
    inputs_act = normal_values(key_of[0], (TOKENS, D), 1.0, 6.0, ((0, 8), (1, 4)))
    out_grad = normal_values(key_of[1], (TOKENS, D), 1.0, 6.0, ((0, 8), (1, 4)))
    pre_act = normal_values(key_of[2], (TOKENS, H), 1.5, 8.0, ((0, 4), (1, 8)))
    w_first = normal_values(key_of[3], (D, H), H ** -0.5, 0.046875, ((0, 4), (1, 8)))
    w_second = normal_values(key_of[4], (H, D), D ** -0.5, 0.09375, ((0, 8), (1, 4)))
    return dict(inputs_act=inputs_act, out_grad=out_grad, pre_act=pre_act, w_first=w_first, w_second=w_second)


gelu_coef = 0.044715

def gelu_pair(pre_float):
    inner_c = math.sqrt(2.0 / math.pi)
    inner = inner_c * (pre_float + gelu_coef * pre_float * pre_float * pre_float)
    tanh_val = jnp.tanh(inner)
    act = 0.5 * pre_float * (1.0 + tanh_val)
    slope = 0.5 * (1.0 + tanh_val) + 0.5 * pre_float * (1.0 - tanh_val * tanh_val) * inner_c * (1.0 + 3.0 * gelu_coef * pre_float * pre_float)
    return (act, slope)

def reference(inputs_act, out_grad, pre_act, w_first, w_second):
    act_float, slope = gelu_pair(pre_act.astype(jnp.float32))
    act = act_float.astype(jnp.bfloat16)
    grad_hidden = lax.dot_general(out_grad, w_second, (((1,), (1,)), ((), ())), preferred_element_type=jnp.float32)
    grad_pre = (grad_hidden * slope).astype(jnp.bfloat16)
    block_width = H // N_ROW

    def add_block(running, block_index):
        start = (block_index * block_width).astype(jnp.int32)
        grad_block = lax.dynamic_slice_in_dim(grad_pre, start, block_width, 1)
        weight_block = lax.dynamic_slice_in_dim(w_first, start, block_width, 1)
        partial_sum = lax.dot_general(grad_block, weight_block, (((1,), (1,)), ((), ())), preferred_element_type=jnp.float32)
        rounded = lax.optimization_barrier(partial_sum.astype(jnp.bfloat16))
        return (running + rounded.astype(jnp.float32), None)
    start_total = jnp.zeros((grad_pre.shape[0], w_first.shape[0]), jnp.float32)
    input_total, unused = lax.scan(add_block, start_total, jnp.arange(N_ROW, dtype=jnp.int32))
    grad_input = input_total.astype(jnp.bfloat16)
    factor = 1.0 / math.sqrt(TOKENS)
    grad_first = lax.dot_general(inputs_act, grad_pre, (((0,), (0,)), ((), ())), preferred_element_type=jnp.float32) * factor
    grad_second = lax.dot_general(act, out_grad, (((0,), (0,)), ((), ())), preferred_element_type=jnp.float32) * factor
    return (grad_input, grad_first, grad_second)
```

```python
import functools
import math

import jax
import jax.numpy as jnp
from jax import lax
from jax.experimental import pallas as pl
from jax.experimental.pallas import tpu as pltpu
from jax.sharding import PartitionSpec as P

gelu_coef = 0.044715
inner_c = math.sqrt(2.0 / math.pi)
STRIP = 16
MESH = pl.DeviceIdType.MESH


def tanh_of(p):
    return jnp.tanh(inner_c * (p + gelu_coef * p * p * p))


def act_of(p):
    return 0.5 * p * (1.0 + tanh_of(p))


def slope_of(p):
    t = tanh_of(p)
    return 0.5 * (1.0 + t) + 0.5 * p * (1.0 - t * t) * inner_c * (1.0 + 3.0 * gelu_coef * p * p)


def contract_last(left, right):
    return lax.dot_general(
        left, right, (((1,), (1,)), ((), ())), preferred_element_type=jnp.float32
    )


def contract_first(left, right):
    return lax.dot_general(
        left, right, (((0,), (0,)), ((), ())), preferred_element_type=jnp.float32
    )


def strips(first, count, body):
    def one(i, carry):
        body(pl.ds(pl.multiple_of(first + i * STRIP, STRIP), STRIP))
        return carry

    lax.fori_loop(0, count // STRIP, one, 0)


def kernel(
    R, N, F, lead, early, skew, factor,
    x_ref, dy_ref, pre_ref, w1_ref, w2_ref,
    gi, gs, gf, act, dy_far,
    w1, w2, dy, x, hid, pre, gp, slope, rs, gi_send, gi_recv,
    loc, dy_s, dy_r, x_s, x_r, fw_s, pr_s, pr_r, rs_s, rs_r, gp_s, gp_r, gi_s, gi_r,
):
    r = lax.axis_index("row")
    c = lax.axis_index("col")
    q = R // N
    Tr = dy_ref.shape[0]
    Tc, H = pre_ref.shape
    Dc = dy_ref.shape[1]
    fine = Tc // F
    per = F // q
    last = N - 1
    f32, bf16 = jnp.float32, jnp.bfloat16

    barrier = pltpu.get_barrier_semaphore()
    for k in range(1, R):
        pl.semaphore_signal(barrier, inc=1, device_id={"row": lax.rem(r + k, R)}, device_id_type=MESH)

    @pl.when(c > 0)
    def _():
        pl.semaphore_signal(barrier, inc=1, device_id={"col": c - 1}, device_id_type=MESH)

    @pl.when(c < last)
    def _():
        pl.semaphore_signal(barrier, inc=1, device_id={"col": c + 1}, device_id_type=MESH)

    local = [
        pltpu.make_async_copy(dy_ref, dy.at[r], loc.at[0]),
        pltpu.make_async_copy(pre_ref, pre.at[c], loc.at[1]),
        pltpu.make_async_copy(w2_ref, w2, loc.at[2]),
        pltpu.make_async_copy(w1_ref, w1, loc.at[3]),
        pltpu.make_async_copy(x_ref, x.at[r], loc.at[4]),
    ]
    for copy in local:
        copy.start()
    ends = jnp.where(c > 0, 1, 0) + jnp.where(c < last, 1, 0)
    pl.semaphore_wait(barrier, R - 1 + ends)

    front = 1 - (2 * c) // N
    back = 1 - front
    far = front * last

    def position(side):
        return c + side * (last - 2 * c)

    def shard_at(side, t):
        return t + side * (last - 2 * t)

    def after(side):
        return c + 1 - 2 * side

    def loop(first, end, body):
        def one(i, carry):
            body(i)
            return carry

        lax.fori_loop(first, end, one, 0)

    def piece(j):
        return pl.ds(pl.multiple_of(j * fine, fine), fine)

    sibling = r + 1 - 2 * lax.rem(r, 2)
    chips = R // 2

    def row_send(src, dst, k, send, recv):
        to = sibling if k == 0 else lax.rem(r + 2 * k, R)
        return pltpu.make_async_remote_copy(
            src_ref=src, dst_ref=dst.at[r], send_sem=send.at[k], recv_sem=recv.at[r],
            device_id={"row": to}, device_id_type=MESH)

    def row_got(src, dst, p, send, recv):
        return pltpu.make_async_remote_copy(
            src_ref=src, dst_ref=dst.at[p], send_sem=send, recv_sem=recv.at[p],
            device_id={"row": sibling}, device_id_type=MESH)

    def row_forward(which, dst, k, recv):
        p = lax.rem(r + 2 * k, R)
        return pltpu.make_async_remote_copy(
            src_ref=dst.at[p], dst_ref=dst.at[p], send_sem=fw_s.at[which, k], recv_sem=recv.at[p],
            device_id={"row": sibling}, device_id_type=MESH)

    def row_start(src, dst, send, recv):
        for k in list(range(1, chips)) + [0]:
            row_send(src, dst, k, send, recv).start()

    def row_pass(which, src, dst, send, recv):
        for k in range(1, chips):
            row_got(src, dst, lax.rem(r + 2 * k, R), send.at[k], recv).wait_recv()
            row_forward(which, dst, k, recv).start()

    def row_rest(src, dst, send, recv):
        for k in range(chips):
            row_got(src, dst, lax.rem(sibling + 2 * k, R), send.at[k], recv).wait_recv()

    def row_end(which, src, dst, send, recv):
        for k in range(chips):
            row_send(src, dst, k, send, recv).wait_send()
            if k > 0:
                row_forward(which, dst, k, recv).wait_send()

    def along(src, dst, side, send, recv):
        return pltpu.make_async_remote_copy(
            src_ref=src, dst_ref=dst, send_sem=send, recv_sem=recv,
            device_id={"col": after(side)}, device_id_type=MESH)

    def pre_copy(side, s, j, src=None):
        place = pre.at[s, piece(j)]
        return along(place if src is None else src, place, side, pr_s.at[side, s], pr_r.at[s, j])

    def gp_copy(side, s, j):
        place = gp.at[s, piece(j)]
        return along(place, place, side, gp_s.at[side, s], gp_r.at[s, j])

    def rs_copy(side, t, j):
        return along(hid.at[shard_at(side, t), piece(j)], rs.at[side, t - 1, piece(j)], side,
                     rs_s.at[side, t - 1], rs_r.at[side, t - 1, j])

    def send_own(side, first, end):
        loop(first, end, lambda j: pre_copy(side, c, j, pre_ref.at[piece(j)]).start())

    row_start(dy_ref, dy, dy_s, dy_r)
    for side in (front, back):
        @pl.when(position(side) < last)
        def _():
            send_own(side, 0, jnp.where(position(side) == 0, lead, F))

    local[1].wait()

    def slope_strip(rows):
        slope[rows, :] = slope_of(pre[c, rows, :].astype(f32))

    def act_rows(s, first, count):
        def one(rows):
            act[s, rows, :] = act_of(pre[s, rows, :].astype(f32)).astype(bf16)

        strips(first, count, one)

    strips(0, Tc, slope_strip)
    act_rows(c, 0, Tc)

    local[0].wait()
    local[2].wait()
    row_pass(0, dy_ref, dy, dy_s, dy_r)
    row_rest(dy_ref, dy, dy_s, dy_r)
    row_start(x_ref, x, x_s, x_r)

    tile_h = min(512, H)

    def partial(k):
        t = last - k
        s = shard_at(back, t)

        def one(i):
            cols = pl.ds(pl.multiple_of(i * tile_h, tile_h), tile_h)
            left = dy[pl.ds(q * s, q)].reshape(Tc, Dc)
            hid[s, :, cols] = contract_last(left, w2[cols, :]).astype(bf16)

        loop(0, H // tile_h, one)

        @pl.when((position(back) == 0) & (t > 0))
        def _():
            loop(0, F, lambda j: rs_copy(back, t, j).start())

    loop(0, N, partial)

    def pre_move(side, t, j):
        s = shard_at(side, t)
        pre_copy(side, s, j).wait_recv()

        @pl.when(position(side) < last)
        def _():
            pre_copy(side, s, j).start()

        act_rows(s, j * fine, fine)

    def both(body):
        def one(jj):
            def turn(u):
                j = jj - u * skew

                @pl.when((j >= 0) & (j < F))
                def _():
                    body(front + u * (back - front), j)

            loop(0, 2, turn)

        return one

    def early_pre(p):
        loop(0, early, lambda j: pre_move(p, 0, j))

    def first_rounds(i):
        @pl.when((i == N - 2) & (position(back) == 1))
        def _():
            early_pre(back)

        @pl.when((i == N - 2) & (position(front) == 1))
        def _():
            early_pre(front)

        def body(side, j):
            p = position(side)

            @pl.when(p > i)
            def _():
                pre_move(side, p - i, j)

            @pl.when((p >= 1) & (p <= i))
            def _():
                t = last - i + p
                s = shard_at(side, t)
                rs_copy(side, t, j).wait_recv()

                def add(rows):
                    total = hid[s, rows, :].astype(f32) + rs[side, t - 1, rows, :].astype(f32)
                    hid[s, rows, :] = total.astype(bf16)

                strips(j * fine, fine, add)
                rs_copy(side, t, j).start()

        loop(0, F + skew, both(body))

    loop(1, N - 1, first_rounds)
    row_pass(1, x_ref, x, x_s, x_r)
    local[3].wait()
    tile_d = min(512, Dc)

    def gi_copy(s, i):
        to = q * s + i
        return pltpu.make_async_remote_copy(
            src_ref=gi_send.at[s, pl.ds(i * Tr, Tr)], dst_ref=gi_recv.at[r],
            send_sem=gi_s.at[to], recv_sem=gi_r.at[r], device_id={"row": to}, device_id_type=MESH)

    def use_rows(s, i):
        rows = pl.ds(pl.multiple_of(i * Tr, Tr), Tr)

        def one(t):
            cols = pl.ds(pl.multiple_of(t * tile_d, tile_d), tile_d)
            gi_send[s, rows, cols] = contract_last(gp[s, rows, :], w1[cols, :]).astype(bf16)

        loop(0, Dc // tile_d, one)
        to = q * s + i

        @pl.when(to != r)
        def _():
            gi_copy(s, i).start()

        @pl.when(to == r)
        def _():
            gi_recv[r] = gi_send[s, rows, :]

    for side in (front, back):
        @pl.when((position(side) >= 2) & (position(side) < last))
        def _():
            early_pre(side)

    def own(j):
        for side in (front, back):
            @pl.when(position(side) > 0)
            def _():
                rs_copy(side, position(side), j).wait_recv()

        up = jnp.maximum(c - 1, 0)
        down = jnp.maximum(last - c - 1, 0)

        def middle(rows):
            total = hid[c, rows, :].astype(f32) + rs[0, up, rows, :].astype(f32)
            total = total + rs[1, down, rows, :].astype(f32)
            gp[c, rows, :] = (total * slope[rows, :]).astype(bf16)

        def edge(rows):
            total = hid[c, rows, :].astype(f32) + rs[front, last - 1, rows, :].astype(f32)
            gp[c, rows, :] = (total * slope[rows, :]).astype(bf16)

        @pl.when(position(back) > 0)
        def _():
            strips(j * fine, fine, middle)

        @pl.when(position(back) == 0)
        def _():
            strips(j * fine, fine, edge)

        for side in (front, back):
            @pl.when(position(side) < last)
            def _():
                gp_copy(side, c, j).start()

        @pl.when(lax.rem(j, per) == per - 1)
        def _():
            use_rows(c, j // per)

    loop(0, F, own)

    @pl.when(position(back) == 0)
    def _():
        send_own(back, lead, F)

    dy_far[...] = dy[pl.ds(q * far, q)].reshape(Tc, Dc)
    row_rest(x_ref, x, x_s, x_r)
    local[4].wait()

    tile_g = H // F

    def gs_tile(i):
        rows = pl.ds(pl.multiple_of(i * tile_g, tile_g), tile_g)
        left = act[pl.ds(back, last), :, rows].reshape(last * Tc, tile_g)
        right = dy[pl.ds(q * back, q * last)].reshape(last * Tc, Dc)
        gs[rows, :] = contract_first(left, right)

    def gf_tile(i):
        cols = pl.ds(pl.multiple_of(i * tile_g, tile_g), tile_g)
        right = gp[:, :, cols].reshape(N * Tc, tile_g)
        gf[:, cols] = contract_first(x[...].reshape(N * Tc, Dc), right) * factor

    def late_rounds(i):
        def body(side, j):
            p = position(side)

            @pl.when(p > i - N)
            def _():
                s = shard_at(side, p - 1 + N - i)
                gp_copy(side, s, j).wait_recv()

                @pl.when(p < last)
                def _():
                    gp_copy(side, s, j).start()

                @pl.when(lax.rem(j, per) == per - 1)
                def _():
                    use_rows(s, j // per)

            @pl.when((p == i - N) & (p >= 1) & (j >= early))
            def _():
                pre_move(side, 0, j)

        step = both(body)

        def one(jj):
            step(jj)

            @pl.when((i == 2 * N - 2) & (jj < F))
            def _():
                gs_tile(jj)

        loop(0, F + skew, one)

    loop(N, 2 * N - 1, late_rounds)

    def finish():
        for k in range(1, R):
            p = lax.rem(r + k, R)
            row_got(gi_send.at[0, pl.ds(0, Tr)], gi_recv, p, gi_s.at[p], gi_r).wait_recv()

        def total_strip(rows):
            total = gi_recv[0, rows, :].astype(f32)
            for p in range(1, R):
                total = total + gi_recv[p, rows, :].astype(f32)
            gi[rows, :] = total.astype(bf16)

        strips(0, Tr, total_strip)

    def last_round(j):
        gf_tile(j)

        @pl.when(j == F - 1)
        def _():
            finish()

        @pl.when(position(front) == last)
        def _():
            pre_move(front, 0, j)

    loop(0, F, last_round)

    row_end(0, dy_ref, dy, dy_s, dy_r)
    row_end(1, x_ref, x, x_s, x_r)
    for s in range(N):
        for i in range(q):
            @pl.when(q * s + i != r)
            def _():
                gi_copy(s, i).wait_send()
    for side in (0, 1):
        p = position(side)
        for t in range(last):
            s = shard_at(side, t)

            @pl.when((p >= t) & (p < last))
            def _():
                along(pre.at[s], pre.at[s], side, pr_s.at[side, s], pr_r.at[s, 0]).wait_send()
                along(gp.at[s], gp.at[s], side, gp_s.at[side, s], gp_r.at[s, 0]).wait_send()

        for t in range(1, N):
            s = shard_at(side, t)

            @pl.when(p < t)
            def _():
                along(hid.at[s], rs.at[side, t - 1], side, rs_s.at[side, t - 1],
                      rs_r.at[side, t - 1, 0]).wait_send()


def exchange(R, N, factor, x, dy, pre, w1, w2):
    Tr, Dc = dy.shape
    Tc, H = pre.shape
    bf16, f32 = jnp.bfloat16, jnp.float32
    dma = pltpu.SemaphoreType.DMA
    F = 8
    hbm = pl.BlockSpec(memory_space=pltpu.HBM)
    vmem = pl.BlockSpec(memory_space=pltpu.VMEM)
    return pl.pallas_call(
        functools.partial(kernel, R, N, F, 6, 1, 2, factor),
        out_shape=[
            pltpu.VMEM((Tr, Dc), bf16),
            pltpu.VMEM((H, Dc), f32),
            pltpu.VMEM((Dc, H), f32),
            pltpu.VMEM((N, Tc, H), bf16),
            pltpu.VMEM((Tc, Dc), bf16),
        ],
        in_specs=[hbm] * 5,
        out_specs=[vmem] * 5,
        scratch_shapes=[
            pltpu.VMEM(w1.shape, bf16),
            pltpu.VMEM(w2.shape, bf16),
            pltpu.VMEM((R, Tr, Dc), bf16),
            pltpu.VMEM((R, Tr, Dc), bf16),
            pltpu.VMEM((N, Tc, H), bf16),
            pltpu.VMEM((N, Tc, H), bf16),
            pltpu.VMEM((N, Tc, H), bf16),
            pltpu.VMEM((Tc, H), f32),
            pltpu.VMEM((2, N - 1, Tc, H), bf16),
            pltpu.VMEM((N, Tc, Dc), bf16),
            pltpu.VMEM((R, Tr, Dc), bf16),
            dma((5,)),
            dma((R // 2,)), dma((R,)), dma((R // 2,)), dma((R,)), dma((2, R // 2)),
            dma((2, N)), dma((N, F)),
            dma((2, N - 1)), dma((2, N - 1, F)),
            dma((2, N)), dma((N, F)),
            dma((R,)), dma((R,)),
        ],
        compiler_params=pltpu.CompilerParams(
            collective_id=0, has_side_effects=True, vmem_limit_bytes=40 * 2**20
        ),
    )(x, dy, pre, w1, w2)


def write_out(N, factor, gi, gs, gf, act, dy_far):
    H, Dc = gs.shape
    tile = min(256, H)
    slots = 4

    def body(gi_ref, gs_ref, gf_ref, act_ref, dy_ref, gi_out, gf_out, gs_out, held, sems, gs_sems):
        far = (1 - (2 * lax.axis_index("col")) // N) * (N - 1)
        whole = [
            pltpu.make_async_copy(gi_ref, gi_out, sems.at[0]),
            pltpu.make_async_copy(gf_ref, gf_out, sems.at[1]),
        ]
        for copy in whole:
            copy.start()

        def copy_of(i):
            rows = pl.ds(i * tile, tile)
            return pltpu.make_async_copy(held.at[i % slots], gs_out.at[rows], gs_sems.at[i % slots])

        for i in range(H // tile):
            rows = pl.ds(i * tile, tile)
            if i >= slots:
                copy_of(i - slots).wait()
            held[i % slots] = (gs_ref[rows, :] + contract_first(act_ref[far, :, rows], dy_ref[...])) * factor
            copy_of(i).start()
        for i in range(max(0, H // tile - slots), H // tile):
            copy_of(i).wait()
        for copy in whole:
            copy.wait()

    vmem = pl.BlockSpec(memory_space=pltpu.VMEM)
    hbm = pl.BlockSpec(memory_space=pltpu.HBM)
    dma = pltpu.SemaphoreType.DMA
    return pl.pallas_call(
        body,
        in_specs=[vmem] * 5,
        out_specs=[hbm] * 3,
        out_shape=[jax.ShapeDtypeStruct(a.shape, a.dtype) for a in (gi, gf, gs)],
        scratch_shapes=[pltpu.VMEM((slots, tile, Dc), jnp.float32), dma((2,)), dma((slots,))],
        compiler_params=pltpu.CompilerParams(vmem_limit_bytes=8 * 2**20),
    )(gi, gs, gf, act, dy_far)


def on_device(R, N, inputs_act, out_grad, pre_act, w_first, w_second):
    total_tokens = pre_act.shape[0] * N
    factor = 1.0 / math.sqrt(total_tokens)
    parts = exchange(R, N, factor, inputs_act, out_grad, pre_act, w_first, w_second)
    return tuple(write_out(N, factor, *parts))


def solution(mesh):
    in_specs = (P("row", "col"), P("row", "col"), P("col", "row"), P("col", "row"), P("row", "col"))
    out_specs = (P("row", "col"), P("col", "row"), P("row", "col"))
    return jax.shard_map(
        functools.partial(on_device, mesh.shape["row"], mesh.shape["col"]),
        mesh=mesh, in_specs=in_specs, out_specs=out_specs, check_vma=False,
    )
```

```python
import functools
import math

import jax
import jax.numpy as jnp
from jax import lax
from jax.experimental import pallas as pl
from jax.experimental.pallas import tpu as pltpu
from jax.sharding import PartitionSpec as P

gelu_coef = 0.044715
inner_c = math.sqrt(2.0 / math.pi)
STRIP = 16
MESH = pl.DeviceIdType.MESH


def tanh_of(p):
    return jnp.tanh(inner_c * (p + gelu_coef * p * p * p))


def act_of(p):
    return 0.5 * p * (1.0 + tanh_of(p))


def slope_of(p):
    t = tanh_of(p)
    return 0.5 * (1.0 + t) + 0.5 * p * (1.0 - t * t) * inner_c * (1.0 + 3.0 * gelu_coef * p * p)


def contract_last(left, right):
    return lax.dot_general(
        left, right, (((1,), (1,)), ((), ())), preferred_element_type=jnp.float32
    )


def contract_first(left, right):
    return lax.dot_general(
        left, right, (((0,), (0,)), ((), ())), preferred_element_type=jnp.float32
    )


def strips(first, count, body):
    def one(i, carry):
        body(pl.ds(pl.multiple_of(first + i * STRIP, STRIP), STRIP))
        return carry

    lax.fori_loop(0, count // STRIP, one, 0)


def kernel(
    R, N, F, lead, head, early, skew, factor,
    x_ref, dy_ref, pre_ref, w1_ref, w2_ref,
    gi, gs, gf, act, dy_far, tail, pre_in, gp_in,
    w1, w2, dy, x, hid, pre, gp, slope, rs, gi_send, gi_recv,
    loc, dy_s, dy_r, x_s, x_r, fw_s, pr_s, pr_r, rs_s, rs_r, gp_s, gp_r, gi_s, gi_r, pre_l, gp_l,
):
    r = lax.axis_index("row")
    c = lax.axis_index("col")
    q = R // N
    Tr = dy_ref.shape[0]
    Tc, H = pre_ref.shape
    Dc = dy_ref.shape[1]
    fine = Tc // F
    per = F // q
    last = N - 1
    f32, bf16 = jnp.float32, jnp.bfloat16

    barrier = pltpu.get_barrier_semaphore()
    for k in range(1, R):
        pl.semaphore_signal(barrier, inc=1, device_id={"row": lax.rem(r + k, R)}, device_id_type=MESH)

    @pl.when(c > 0)
    def _():
        pl.semaphore_signal(barrier, inc=1, device_id={"col": c - 1}, device_id_type=MESH)

    @pl.when(c < last)
    def _():
        pl.semaphore_signal(barrier, inc=1, device_id={"col": c + 1}, device_id_type=MESH)

    local = [
        pltpu.make_async_copy(dy_ref, dy.at[r], loc.at[0]),
        pltpu.make_async_copy(pre_ref, pre.at[c], loc.at[1]),
        pltpu.make_async_copy(w2_ref, w2, loc.at[2]),
        pltpu.make_async_copy(w1_ref, w1, loc.at[3]),
        pltpu.make_async_copy(x_ref, x.at[r], loc.at[4]),
    ]
    for copy in local:
        copy.start()
    ends = jnp.where(c > 0, 1, 0) + jnp.where(c < last, 1, 0)
    pl.semaphore_wait(barrier, R - 1 + ends)

    front = 1 - (2 * c) // N
    back = 1 - front
    far = front * last

    def position(side):
        return c + side * (last - 2 * c)

    def shard_at(side, t):
        return t + side * (last - 2 * t)

    def after(side):
        return c + 1 - 2 * side

    def loop(first, end, body):
        def one(i, carry):
            body(i)
            return carry

        lax.fori_loop(first, end, one, 0)

    def piece(j):
        return pl.ds(pl.multiple_of(j * fine, fine), fine)

    sibling = r + 1 - 2 * lax.rem(r, 2)
    chips = R // 2

    def row_send(src, dst, k, send, recv):
        to = sibling if k == 0 else lax.rem(r + 2 * k, R)
        return pltpu.make_async_remote_copy(
            src_ref=src, dst_ref=dst.at[r], send_sem=send.at[k], recv_sem=recv.at[r],
            device_id={"row": to}, device_id_type=MESH)

    def row_got(src, dst, p, send, recv):
        return pltpu.make_async_remote_copy(
            src_ref=src, dst_ref=dst.at[p], send_sem=send, recv_sem=recv.at[p],
            device_id={"row": sibling}, device_id_type=MESH)

    def row_forward(which, dst, k, recv):
        p = lax.rem(r + 2 * k, R)
        return pltpu.make_async_remote_copy(
            src_ref=dst.at[p], dst_ref=dst.at[p], send_sem=fw_s.at[which, k], recv_sem=recv.at[p],
            device_id={"row": sibling}, device_id_type=MESH)

    def row_start(src, dst, send, recv):
        for k in list(range(1, chips)) + [0]:
            row_send(src, dst, k, send, recv).start()

    def row_pass(which, src, dst, send, recv):
        for k in range(1, chips):
            row_got(src, dst, lax.rem(r + 2 * k, R), send.at[k], recv).wait_recv()
            row_forward(which, dst, k, recv).start()

    def row_rest(src, dst, send, recv):
        for k in range(chips):
            row_got(src, dst, lax.rem(sibling + 2 * k, R), send.at[k], recv).wait_recv()

    def row_end(which, src, dst, send, recv):
        for k in range(chips):
            row_send(src, dst, k, send, recv).wait_send()
            if k > 0:
                row_forward(which, dst, k, recv).wait_send()

    def along(src, dst, side, send, recv):
        return pltpu.make_async_remote_copy(
            src_ref=src, dst_ref=dst, send_sem=send, recv_sem=recv,
            device_id={"col": after(side)}, device_id_type=MESH)

    def pre_copy(side, s, j, src=None):
        place = pre_in.at[s, piece(j)]
        return along(place if src is None else src, place, side, pr_s.at[side, s], pr_r.at[s, j])

    def pre_last(side, s, src=None):
        place = tail.at[s]
        return along(place if src is None else src, place, side, pr_s.at[side, s], pr_r.at[s, F - 1])

    def pre_load(side, s, j):
        return pltpu.make_async_copy(pre_in.at[s, piece(j)], pre.at[s, piece(j)], pre_l.at[side, j])

    def gp_copy(side, s, j, src=None):
        place = gp_in.at[s, piece(j)]
        return along(place if src is None else src, place, side, gp_s.at[side, s], gp_r.at[s, j])

    def gp_load(side, s, j):
        return pltpu.make_async_copy(gp_in.at[s, piece(j)], gp.at[s, piece(j)], gp_l.at[side, j])

    def rs_copy(side, t, j):
        return along(hid.at[shard_at(side, t), piece(j)], rs.at[side, t - 1, piece(j)], side,
                     rs_s.at[side, t - 1], rs_r.at[side, t - 1, j])

    def send_own(side, first, end):
        loop(first, end, lambda j: pre_copy(side, c, j, pre_ref.at[piece(j)]).start())

    def send_own_last(side):
        pre_last(side, c, pre_ref.at[piece(F - 1)]).start()

    for side in (front, back):
        @pl.when((position(side) < last) & (position(side) > 0))
        def _():
            send_own(side, 0, F - 1)
            send_own_last(side)

        @pl.when(position(side) == 0)
        def _():
            send_own(side, 0, lead)
    row_start(dy_ref, dy, dy_s, dy_r)

    local[1].wait()

    def slope_strip(rows):
        slope[rows, :] = slope_of(pre[c, rows, :].astype(f32))

    def act_rows(s, first, count):
        def one(rows):
            act[s, rows, :] = act_of(pre[s, rows, :].astype(f32)).astype(bf16)

        strips(first, count, one)

    strips(0, Tc, slope_strip)
    act_rows(c, 0, Tc)

    def pre_move(side, t, j):
        s = shard_at(side, t)

        @pl.when(j < F - 1)
        def _():
            pre_copy(side, s, j).wait_recv()

            @pl.when(position(side) < last)
            def _():
                pre_copy(side, s, j).start()

            pre_load(side, s, j).start()

        @pl.when(j == F - 1)
        def _():
            pre_last(side, s).wait_recv()

            @pl.when(position(side) < last)
            def _():
                pre_last(side, s).start()

    def pre_use(side, t, j):
        s = shard_at(side, t)

        @pl.when(j < F - 1)
        def _():
            pre_load(side, s, j).wait()
            act_rows(s, j * fine, fine)

        @pl.when((j == F - 1) & (s != far))
        def _():
            def one(i):
                rows = pl.ds(pl.multiple_of(i * STRIP, STRIP), STRIP)
                act[s, pl.ds(pl.multiple_of((F - 1) * fine + i * STRIP, STRIP), STRIP), :] = act_of(
                    tail[s, rows, :].astype(f32)).astype(bf16)

            loop(0, fine // STRIP, one)

    def next_pre(first, end):
        @pl.when(position(front) > 1)
        def _():
            loop(first, end, lambda j: pre_move(front, position(front) - 1, j))

        @pl.when(position(back) > 1)
        def _():
            loop(first, end, lambda j: pre_move(back, position(back) - 1, j))

    next_pre(0, head)

    local[0].wait()
    local[2].wait()
    row_pass(0, dy_ref, dy, dy_s, dy_r)
    row_rest(dy_ref, dy, dy_s, dy_r)
    row_start(x_ref, x, x_s, x_r)

    tile_h = min(512, H)

    def partial(k):
        t = last - k
        s = shard_at(back, t)

        def one(i):
            cols = pl.ds(pl.multiple_of(i * tile_h, tile_h), tile_h)
            left = dy[pl.ds(q * s, q)].reshape(Tc, Dc)
            hid[s, :, cols] = contract_last(left, w2[cols, :]).astype(bf16)

        loop(0, H // tile_h, one)

        @pl.when((position(back) == 0) & (t > 0))
        def _():
            loop(0, F, lambda j: rs_copy(back, t, j).start())

        next_pre(jnp.minimum(head + k, F), jnp.minimum(head + k + 1, F))

    loop(0, N, partial)

    def both(body):
        def one(jj):
            def turn(u):
                j = jj - u * skew

                @pl.when((j >= 0) & (j < F))
                def _():
                    body(front + u * (back - front), j)

            loop(0, 2, turn)

        return one

    def early_pre(side):
        loop(0, early, lambda j: pre_move(side, 0, j))
        loop(0, early, lambda j: pre_use(side, 0, j))

    def first_rounds(i):
        for side in (front, back):
            p = position(side)

            @pl.when(((i == max(N - 3, 1)) & (p == 1)) | ((i == N - 2) & (p >= 2) & (p < last)))
            def _():
                early_pre(side)

        def body(side, j):
            p = position(side)

            @pl.when((p > i) & ((i > 1) | (j >= head + N)))
            def _():
                pre_move(side, p - i, j)

            @pl.when((p >= 1) & (p <= i))
            def _():
                t = last - i + p
                s = shard_at(side, t)
                rs_copy(side, t, j).wait_recv()

                def add(rows):
                    total = hid[s, rows, :].astype(f32) + rs[side, t - 1, rows, :].astype(f32)
                    hid[s, rows, :] = total.astype(bf16)

                strips(j * fine, fine, add)
                rs_copy(side, t, j).start()

        loop(0, F + skew, both(body))

        def use(u):
            side = front + u * (back - front)
            p = position(side)

            @pl.when(p > i)
            def _():
                loop(0, F, lambda j: pre_use(side, p - i, j))

        loop(0, 2, use)

    loop(1, N - 1, first_rounds)
    row_pass(1, x_ref, x, x_s, x_r)
    local[3].wait()
    tile_d = min(512, Dc)

    def gi_copy(s, i):
        to = q * s + i
        return pltpu.make_async_remote_copy(
            src_ref=gi_send.at[s, pl.ds(i * Tr, Tr)], dst_ref=gi_recv.at[r],
            send_sem=gi_s.at[to], recv_sem=gi_r.at[r], device_id={"row": to}, device_id_type=MESH)

    def use_rows(s, i):
        rows = pl.ds(pl.multiple_of(i * Tr, Tr), Tr)

        def one(t):
            cols = pl.ds(pl.multiple_of(t * tile_d, tile_d), tile_d)
            gi_send[s, rows, cols] = contract_last(gp[s, rows, :], w1[cols, :]).astype(bf16)

        loop(0, Dc // tile_d, one)
        to = q * s + i

        @pl.when(to != r)
        def _():
            gi_copy(s, i).start()

        @pl.when(to == r)
        def _():
            gi_recv[r] = gi_send[s, rows, :]

    def own(j):
        for side in (front, back):
            @pl.when(position(side) > 0)
            def _():
                rs_copy(side, position(side), j).wait_recv()

        up = jnp.maximum(c - 1, 0)
        down = jnp.maximum(last - c - 1, 0)

        def middle(rows):
            total = hid[c, rows, :].astype(f32) + rs[0, up, rows, :].astype(f32)
            total = total + rs[1, down, rows, :].astype(f32)
            gp[c, rows, :] = (total * slope[rows, :]).astype(bf16)

        def edge(rows):
            total = hid[c, rows, :].astype(f32) + rs[front, last - 1, rows, :].astype(f32)
            gp[c, rows, :] = (total * slope[rows, :]).astype(bf16)

        @pl.when(position(back) > 0)
        def _():
            strips(j * fine, fine, middle)

        @pl.when(position(back) == 0)
        def _():
            strips(j * fine, fine, edge)

        for side in (front, back):
            @pl.when(position(side) < last)
            def _():
                gp_copy(side, c, j, gp.at[c, piece(j)]).start()

        @pl.when(lax.rem(j, per) == per - 1)
        def _():
            use_rows(c, j // per)

    loop(0, F, own)

    @pl.when(position(back) == 0)
    def _():
        send_own(back, lead, F - 1)
        send_own_last(back)

    dy_far[...] = dy[pl.ds(q * far, q)].reshape(Tc, Dc)
    row_rest(x_ref, x, x_s, x_r)
    local[4].wait()

    tile_g = H // F

    def gs_tile(i):
        rows = pl.ds(pl.multiple_of(i * tile_g, tile_g), tile_g)
        left = act[pl.ds(back, last), :, rows].reshape(last * Tc, tile_g)
        right = dy[pl.ds(q * back, q * last)].reshape(last * Tc, Dc)
        gs[rows, :] = contract_first(left, right)

    def gf_tile(i):
        cols = pl.ds(pl.multiple_of(i * tile_g, tile_g), tile_g)
        right = gp[:, :, cols].reshape(N * Tc, tile_g)
        gf[:, cols] = contract_first(x[...].reshape(N * Tc, Dc), right) * factor

    def late_rounds(i):
        def body(side, j):
            p = position(side)

            @pl.when(p > i - N)
            def _():
                s = shard_at(side, p - 1 + N - i)
                gp_copy(side, s, j).wait_recv()

                @pl.when(p < last)
                def _():
                    gp_copy(side, s, j).start()

                gp_load(side, s, j).start()

                @pl.when(lax.rem(j, per) == per - 1)
                def _():
                    loop(j - per + 1, j + 1, lambda k: gp_load(side, s, k).wait())
                    use_rows(s, j // per)

            @pl.when((p == i - N) & (p >= 1) & (j >= early))
            def _():
                pre_move(side, 0, j)

        step = both(body)

        def one(jj):
            step(jj)

            @pl.when((i == 2 * N - 2) & (jj < F))
            def _():
                gs_tile(jj)

        loop(0, F + skew, one)

        def use(u):
            side = front + u * (back - front)
            p = position(side)

            @pl.when((p == i - N) & (p >= 1))
            def _():
                loop(early, F, lambda j: pre_use(side, 0, j))

        loop(0, 2, use)

    loop(N, 2 * N - 1, late_rounds)

    def finish():
        for k in range(1, R):
            p = lax.rem(r + k, R)
            row_got(gi_send.at[0, pl.ds(0, Tr)], gi_recv, p, gi_s.at[p], gi_r).wait_recv()

        def total_strip(rows):
            total = gi_recv[0, rows, :].astype(f32)
            for p in range(1, R):
                total = total + gi_recv[p, rows, :].astype(f32)
            gi[rows, :] = total.astype(bf16)

        strips(0, Tr, total_strip)

    def sent():
        row_end(0, dy_ref, dy, dy_s, dy_r)
        row_end(1, x_ref, x, x_s, x_r)
        for s in range(N):
            for i in range(q):
                @pl.when(q * s + i != r)
                def _():
                    gi_copy(s, i).wait_send()
        for side in (0, 1):
            p = position(side)
            for t in range(last):
                s = shard_at(side, t)

                @pl.when((p >= t) & (p < last))
                def _():
                    along(pre_in.at[s], pre_in.at[s], side, pr_s.at[side, s], pr_r.at[s, 0]).wait_send()
                    along(gp_in.at[s], gp_in.at[s], side, gp_s.at[side, s], gp_r.at[s, 0]).wait_send()

            for t in range(1, N):
                s = shard_at(side, t)

                @pl.when(p < t)
                def _():
                    along(hid.at[s], rs.at[side, t - 1], side, rs_s.at[side, t - 1],
                          rs_r.at[side, t - 1, 0]).wait_send()

    def last_round(j):
        @pl.when((position(front) == last) & (j < F - 1))
        def _():
            pre_move(front, 0, j)

        gf_tile(j)

        @pl.when((position(front) == last) & (j < F - 1))
        def _():
            pre_use(front, 0, j)

    loop(0, F, last_round)
    finish()
    sent()

    @pl.when(position(front) == last)
    def _():
        pre_move(front, 0, F - 1)


def exchange(R, N, factor, x, dy, pre, w1, w2):
    Tr, Dc = dy.shape
    Tc, H = pre.shape
    bf16, f32 = jnp.bfloat16, jnp.float32
    dma = pltpu.SemaphoreType.DMA
    F = 4
    hbm = pl.BlockSpec(memory_space=pltpu.HBM)
    vmem = pl.BlockSpec(memory_space=pltpu.VMEM)
    return pl.pallas_call(
        functools.partial(kernel, R, N, F, 3, 2, 1, 1, factor),
        out_shape=[
            pltpu.VMEM((Tr, Dc), bf16),
            pltpu.VMEM((H, Dc), f32),
            pltpu.VMEM((Dc, H), f32),
            pltpu.VMEM((N, Tc, H), bf16),
            pltpu.VMEM((Tc, Dc), bf16),
            pltpu.VMEM((N, Tc // F, H), bf16),
            jax.ShapeDtypeStruct((N, Tc, H), bf16),
            jax.ShapeDtypeStruct((N, Tc, H), bf16),
        ],
        in_specs=[hbm] * 5,
        out_specs=[vmem] * 6 + [hbm] * 2,
        scratch_shapes=[
            pltpu.VMEM(w1.shape, bf16),
            pltpu.VMEM(w2.shape, bf16),
            pltpu.VMEM((R, Tr, Dc), bf16),
            pltpu.VMEM((R, Tr, Dc), bf16),
            pltpu.VMEM((N, Tc, H), bf16),
            pltpu.VMEM((N, Tc, H), bf16),
            pltpu.VMEM((N, Tc, H), bf16),
            pltpu.VMEM((Tc, H), f32),
            pltpu.VMEM((2, N - 1, Tc, H), bf16),
            pltpu.VMEM((N, Tc, Dc), bf16),
            pltpu.VMEM((R, Tr, Dc), bf16),
            dma((5,)),
            dma((R // 2,)), dma((R,)), dma((R // 2,)), dma((R,)), dma((2, R // 2)),
            dma((2, N)), dma((N, F)),
            dma((2, N - 1)), dma((2, N - 1, F)),
            dma((2, N)), dma((N, F)),
            dma((R,)), dma((R,)), dma((2, F)), dma((2, F)),
        ],
        compiler_params=pltpu.CompilerParams(
            collective_id=0, has_side_effects=True, vmem_limit_bytes=40 * 2**20
        ),
    )(x, dy, pre, w1, w2)[:6]


def write_out(N, factor, gi, gs, gf, act, dy_far, tail):
    H, Dc = gs.shape
    Tc, fine = act.shape[1], tail.shape[1]
    tile = min(256, H)
    slots = 8

    def body(gi_ref, gs_ref, gf_ref, act_ref, dy_ref, tail_ref, gi_out, gf_out, gs_out, held, end, sems, gs_sems):
        far = (1 - (2 * lax.axis_index("col")) // N) * (N - 1)
        whole = [
            pltpu.make_async_copy(gi_ref, gi_out, sems.at[0]),
            pltpu.make_async_copy(gf_ref, gf_out, sems.at[1]),
        ]
        for copy in whole:
            copy.start()

        def act_strip(rows):
            end[rows, :] = act_of(tail_ref[far, rows, :].astype(jnp.float32)).astype(jnp.bfloat16)

        strips(0, fine, act_strip)

        def copy_of(i):
            rows = pl.ds(i * tile, tile)
            return pltpu.make_async_copy(held.at[i % slots], gs_out.at[rows], gs_sems.at[i % slots])

        for i in range(H // tile):
            rows = pl.ds(i * tile, tile)
            if i >= slots:
                copy_of(i - slots).wait()
            term = contract_first(act_ref[far, 0 : Tc - fine, rows], dy_ref[0 : Tc - fine, :])
            term = term + contract_first(end[:, rows], dy_ref[Tc - fine :, :])
            held[i % slots] = (gs_ref[rows, :] + term) * factor
            copy_of(i).start()
        for i in range(max(0, H // tile - slots), H // tile):
            copy_of(i).wait()
        for copy in whole:
            copy.wait()

    vmem = pl.BlockSpec(memory_space=pltpu.VMEM)
    hbm = pl.BlockSpec(memory_space=pltpu.HBM)
    dma = pltpu.SemaphoreType.DMA
    return pl.pallas_call(
        body,
        in_specs=[vmem] * 6,
        out_specs=[hbm] * 3,
        out_shape=[jax.ShapeDtypeStruct(a.shape, a.dtype) for a in (gi, gf, gs)],
        scratch_shapes=[
            pltpu.VMEM((slots, tile, Dc), jnp.float32), pltpu.VMEM((fine, H), jnp.bfloat16), dma((2,)), dma((slots,)),
        ],
        compiler_params=pltpu.CompilerParams(vmem_limit_bytes=16 * 2**20),
    )(gi, gs, gf, act, dy_far, tail)


def on_device(R, N, inputs_act, out_grad, pre_act, w_first, w_second):
    total_tokens = pre_act.shape[0] * N
    factor = 1.0 / math.sqrt(total_tokens)
    parts = exchange(R, N, factor, inputs_act, out_grad, pre_act, w_first, w_second)
    return tuple(write_out(N, factor, *parts))


def solution(mesh):
    in_specs = (P("row", "col"), P("row", "col"), P("col", "row"), P("col", "row"), P("row", "col"))
    out_specs = (P("row", "col"), P("col", "row"), P("row", "col"))
    return jax.shard_map(
        functools.partial(on_device, mesh.shape["row"], mesh.shape["col"]),
        mesh=mesh, in_specs=in_specs, out_specs=out_specs, check_vma=False,
    )
```

```python
import functools
import math

import jax
import jax.numpy as jnp
from jax import lax
from jax.experimental import pallas as pl
from jax.experimental.pallas import tpu as pltpu
from jax.sharding import PartitionSpec as P

gelu_coef = 0.044715
inner_c = math.sqrt(2.0 / math.pi)
STRIP = 16
MESH = pl.DeviceIdType.MESH


def tanh_of(p):
    return jnp.tanh(inner_c * (p + gelu_coef * p * p * p))


def act_of(p):
    return 0.5 * p * (1.0 + tanh_of(p))


def slope_of(p):
    t = tanh_of(p)
    return 0.5 * (1.0 + t) + 0.5 * p * (1.0 - t * t) * inner_c * (1.0 + 3.0 * gelu_coef * p * p)


def contract_last(left, right):
    return lax.dot_general(
        left, right, (((1,), (1,)), ((), ())), preferred_element_type=jnp.float32
    )


def contract_first(left, right):
    return lax.dot_general(
        left, right, (((0,), (0,)), ((), ())), preferred_element_type=jnp.float32
    )


def strips(first, count, body):
    def one(i, carry):
        body(pl.ds(pl.multiple_of(first + i * STRIP, STRIP), STRIP))
        return carry

    lax.fori_loop(0, count // STRIP, one, 0)


def kernel(
    R, N, F, lead, head, early, skew, factor,
    x_ref, dy_ref, pre_ref, w1_ref, w2_ref,
    gi, gs, gf, act, dy_far, tail, pre_in, gp_in,
    w1, w2, dy, x, hid, pre, gp, slope, rs, gi_send, gi_recv,
    loc, dy_s, dy_r, x_s, x_r, fw_s, pr_s, pr_r, rs_s, rs_r, gp_s, gp_r, gi_s, gi_r, pre_l, gp_l, rl_s, rl_r,
):
    r = lax.axis_index("row")
    c = lax.axis_index("col")
    q = R // N
    Tr = dy_ref.shape[0]
    Tc, H = pre_ref.shape
    Dc = dy_ref.shape[1]
    fine = Tc // F
    per = F // q
    last = N - 1
    f32, bf16 = jnp.float32, jnp.bfloat16

    sibling = r + 1 - 2 * lax.rem(r, 2)
    chips = R // 2
    square = chips == 4
    beside = r + 2 - 4 * lax.rem(r // 2, 2)
    across = lax.rem(r + 4, R)
    corner = lax.rem(beside + 4, R)

    barrier = pltpu.get_barrier_semaphore()
    greeted = [sibling, beside, across] if square else [lax.rem(r + k, R) for k in range(1, R)]
    for peer in greeted:
        pl.semaphore_signal(barrier, inc=1, device_id={"row": peer}, device_id_type=MESH)

    @pl.when(c > 0)
    def _():
        pl.semaphore_signal(barrier, inc=1, device_id={"col": c - 1}, device_id_type=MESH)

    @pl.when(c < last)
    def _():
        pl.semaphore_signal(barrier, inc=1, device_id={"col": c + 1}, device_id_type=MESH)

    local = [
        pltpu.make_async_copy(dy_ref, dy.at[r], loc.at[0]),
        pltpu.make_async_copy(pre_ref, pre.at[c], loc.at[1]),
        pltpu.make_async_copy(w2_ref, w2, loc.at[2]),
        pltpu.make_async_copy(w1_ref, w1, loc.at[3]),
        pltpu.make_async_copy(x_ref, x.at[r], loc.at[4]),
    ]
    for copy in local:
        copy.start()
    ends = jnp.where(c > 0, 1, 0) + jnp.where(c < last, 1, 0)
    pl.semaphore_wait(barrier, len(greeted) + ends)

    front = 1 - (2 * c) // N
    back = 1 - front
    far = front * last

    def position(side):
        return c + side * (last - 2 * c)

    def shard_at(side, t):
        return t + side * (last - 2 * t)

    def after(side):
        return c + 1 - 2 * side

    def loop(first, end, body):
        def one(i, carry):
            body(i)
            return carry

        lax.fori_loop(first, end, one, 0)

    def piece(j):
        return pl.ds(pl.multiple_of(j * fine, fine), fine)

    def row_send(src, dst, k, send, recv):
        to = sibling if k == 0 else lax.rem(r + 2 * k, R)
        return pltpu.make_async_remote_copy(
            src_ref=src, dst_ref=dst.at[r], send_sem=send.at[k], recv_sem=recv.at[r],
            device_id={"row": to}, device_id_type=MESH)

    def row_got(src, dst, p, send, recv):
        return pltpu.make_async_remote_copy(
            src_ref=src, dst_ref=dst.at[p], send_sem=send, recv_sem=recv.at[p],
            device_id={"row": sibling}, device_id_type=MESH)

    def row_forward(which, dst, k, recv):
        p = lax.rem(r + 2 * k, R)
        return pltpu.make_async_remote_copy(
            src_ref=dst.at[p], dst_ref=dst.at[p], send_sem=fw_s.at[which, k], recv_sem=recv.at[p],
            device_id={"row": sibling}, device_id_type=MESH)

    def row_start(src, dst, send, recv):
        for k in list(range(1, chips)) + [0]:
            row_send(src, dst, k, send, recv).start()

    def row_pass(which, src, dst, send, recv):
        for k in range(1, chips):
            row_got(src, dst, lax.rem(r + 2 * k, R), send.at[k], recv).wait_recv()
            row_forward(which, dst, k, recv).start()

    def row_rest(src, dst, send, recv):
        for k in range(chips):
            row_got(src, dst, lax.rem(sibling + 2 * k, R), send.at[k], recv).wait_recv()

    def row_end(which, src, dst, send, recv):
        for k in range(chips):
            row_send(src, dst, k, send, recv).wait_send()
            if k > 0:
                row_forward(which, dst, k, recv).wait_send()

    half = Tr // 2

    def to_row(src, dst, to, send, recv):
        return pltpu.make_async_remote_copy(
            src_ref=src, dst_ref=dst, send_sem=send, recv_sem=recv, device_id={"row": to}, device_id_type=MESH)

    def dy_own(slot):
        return to_row(dy_ref, dy.at[r], (sibling, beside, across)[slot], dy_s.at[slot], dy_r.at[r])

    def dy_share(slot):
        p = (beside, across, corner)[slot]
        return to_row(dy.at[p], dy.at[p], sibling, fw_s.at[0, slot], dy_r.at[p])

    def dy_got(p):
        to_row(dy_ref, dy.at[p], sibling, dy_s.at[0], dy_r.at[p]).wait_recv()

    def dy_relay(slot):
        place = dy.at[(beside, across)[slot], pl.ds(slot * half, half)]
        return to_row(place, place, (across, beside)[slot], rl_s.at[slot], rl_r.at[slot])

    def dy_corner(slot):
        place = dy.at[corner, pl.ds(slot * half, half)]
        to_row(place, place, sibling, rl_s.at[slot], rl_r.at[slot]).wait_recv()

    def dy_start():
        if not square:
            row_start(dy_ref, dy, dy_s, dy_r)
            return
        for slot in (1, 2, 0):
            dy_own(slot).start()

    def dy_gather():
        if not square:
            row_pass(0, dy_ref, dy, dy_s, dy_r)
            row_rest(dy_ref, dy, dy_s, dy_r)
            return
        for slot in range(2):
            dy_got((beside, across)[slot])
            dy_relay(slot).start()
            dy_share(slot).start()
        for slot in range(2):
            dy_corner(slot)
        dy_share(2).start()
        for k in range(chips):
            dy_got(lax.rem(sibling + 2 * k, R))

    def dy_end():
        if not square:
            row_end(0, dy_ref, dy, dy_s, dy_r)
            return
        for slot in range(3):
            dy_own(slot).wait_send()
            dy_share(slot).wait_send()
        for slot in range(2):
            dy_relay(slot).wait_send()

    def along(src, dst, side, send, recv):
        return pltpu.make_async_remote_copy(
            src_ref=src, dst_ref=dst, send_sem=send, recv_sem=recv,
            device_id={"col": after(side)}, device_id_type=MESH)

    def pre_copy(side, s, j, src=None):
        place = pre_in.at[s, piece(j)]
        return along(place if src is None else src, place, side, pr_s.at[side, s], pr_r.at[s, j])

    def pre_last(side, s, src=None):
        place = tail.at[s]
        return along(place if src is None else src, place, side, pr_s.at[side, s], pr_r.at[s, F - 1])

    def pre_load(side, s, j):
        return pltpu.make_async_copy(pre_in.at[s, piece(j)], pre.at[s, piece(j)], pre_l.at[side, j])

    def gp_copy(side, s, j, src=None):
        place = gp_in.at[s, piece(j)]
        return along(place if src is None else src, place, side, gp_s.at[side, s], gp_r.at[s, j])

    def gp_load(side, s, j):
        return pltpu.make_async_copy(gp_in.at[s, piece(j)], gp.at[s, piece(j)], gp_l.at[side, j])

    def rs_copy(side, t, j):
        return along(hid.at[shard_at(side, t), piece(j)], rs.at[side, t - 1, piece(j)], side,
                     rs_s.at[side, t - 1], rs_r.at[side, t - 1, j])

    def send_own(side, first, end):
        loop(first, end, lambda j: pre_copy(side, c, j, pre_ref.at[piece(j)]).start())

    def send_own_last(side):
        pre_last(side, c, pre_ref.at[piece(F - 1)]).start()

    for side in (front, back):
        @pl.when((position(side) < last) & (position(side) > 0))
        def _():
            send_own(side, 0, F - 1)
            send_own_last(side)

        @pl.when(position(side) == 0)
        def _():
            send_own(side, 0, lead)
    dy_start()

    local[1].wait()

    def slope_strip(rows):
        slope[rows, :] = slope_of(pre[c, rows, :].astype(f32))

    def act_rows(s, first, count):
        def one(rows):
            act[s, rows, :] = act_of(pre[s, rows, :].astype(f32)).astype(bf16)

        strips(first, count, one)

    strips(0, Tc, slope_strip)
    act_rows(c, 0, Tc)

    def pre_move(side, t, j):
        s = shard_at(side, t)

        @pl.when(j < F - 1)
        def _():
            pre_copy(side, s, j).wait_recv()

            @pl.when(position(side) < last)
            def _():
                pre_copy(side, s, j).start()

            pre_load(side, s, j).start()

        @pl.when(j == F - 1)
        def _():
            pre_last(side, s).wait_recv()

            @pl.when(position(side) < last)
            def _():
                pre_last(side, s).start()

    def pre_use(side, t, j):
        s = shard_at(side, t)

        @pl.when(j < F - 1)
        def _():
            pre_load(side, s, j).wait()
            act_rows(s, j * fine, fine)

        @pl.when((j == F - 1) & (s != far))
        def _():
            def one(i):
                rows = pl.ds(pl.multiple_of(i * STRIP, STRIP), STRIP)
                act[s, pl.ds(pl.multiple_of((F - 1) * fine + i * STRIP, STRIP), STRIP), :] = act_of(
                    tail[s, rows, :].astype(f32)).astype(bf16)

            loop(0, fine // STRIP, one)

    def next_pre(first, end):
        @pl.when(position(front) > 1)
        def _():
            loop(first, end, lambda j: pre_move(front, position(front) - 1, j))

        @pl.when(position(back) > 1)
        def _():
            loop(first, end, lambda j: pre_move(back, position(back) - 1, j))

    next_pre(0, head)

    local[0].wait()
    local[2].wait()
    dy_gather()
    row_start(x_ref, x, x_s, x_r)

    tile_h = min(512, H)

    def partial(k):
        t = last - k
        s = shard_at(back, t)

        def one(i):
            cols = pl.ds(pl.multiple_of(i * tile_h, tile_h), tile_h)
            left = dy[pl.ds(q * s, q)].reshape(Tc, Dc)
            hid[s, :, cols] = contract_last(left, w2[cols, :]).astype(bf16)

        loop(0, H // tile_h, one)

        @pl.when((position(back) == 0) & (t > 0))
        def _():
            loop(0, F, lambda j: rs_copy(back, t, j).start())

        next_pre(jnp.minimum(head + k, F), jnp.minimum(head + k + 1, F))

    loop(0, N, partial)

    def both(body):
        def one(jj):
            def turn(u):
                j = jj - u * skew

                @pl.when((j >= 0) & (j < F))
                def _():
                    body(front + u * (back - front), j)

            loop(0, 2, turn)

        return one

    def early_pre(side):
        loop(0, early, lambda j: pre_move(side, 0, j))
        loop(0, early, lambda j: pre_use(side, 0, j))

    def first_rounds(i):
        for side in (front, back):
            p = position(side)

            @pl.when(((i == max(N - 3, 1)) & (p == 1)) | ((i == N - 2) & (p >= 2) & (p < last)))
            def _():
                early_pre(side)

        def body(side, j):
            p = position(side)

            @pl.when((p > i) & ((i > 1) | (j >= head + N)))
            def _():
                pre_move(side, p - i, j)

            @pl.when((p >= 1) & (p <= i))
            def _():
                t = last - i + p
                s = shard_at(side, t)
                rs_copy(side, t, j).wait_recv()

                def add(rows):
                    total = hid[s, rows, :].astype(f32) + rs[side, t - 1, rows, :].astype(f32)
                    hid[s, rows, :] = total.astype(bf16)

                strips(j * fine, fine, add)
                rs_copy(side, t, j).start()

        loop(0, F + skew, both(body))

        def use(u):
            side = front + u * (back - front)
            p = position(side)

            @pl.when(p > i)
            def _():
                loop(0, F, lambda j: pre_use(side, p - i, j))

        loop(0, 2, use)

    loop(1, N - 1, first_rounds)
    row_pass(1, x_ref, x, x_s, x_r)
    local[3].wait()
    tile_d = min(512, Dc)

    def gi_copy(s, i):
        to = q * s + i
        return pltpu.make_async_remote_copy(
            src_ref=gi_send.at[s, pl.ds(i * Tr, Tr)], dst_ref=gi_recv.at[r],
            send_sem=gi_s.at[to], recv_sem=gi_r.at[r], device_id={"row": to}, device_id_type=MESH)

    def use_rows(s, i):
        rows = pl.ds(pl.multiple_of(i * Tr, Tr), Tr)

        def one(t):
            cols = pl.ds(pl.multiple_of(t * tile_d, tile_d), tile_d)
            gi_send[s, rows, cols] = contract_last(gp[s, rows, :], w1[cols, :]).astype(bf16)

        loop(0, Dc // tile_d, one)
        to = q * s + i

        @pl.when(to != r)
        def _():
            gi_copy(s, i).start()

        @pl.when(to == r)
        def _():
            gi_recv[r] = gi_send[s, rows, :]

    def own(j):
        for side in (front, back):
            @pl.when(position(side) > 0)
            def _():
                rs_copy(side, position(side), j).wait_recv()

        up = jnp.maximum(c - 1, 0)
        down = jnp.maximum(last - c - 1, 0)

        def middle(rows):
            total = hid[c, rows, :].astype(f32) + rs[0, up, rows, :].astype(f32)
            total = total + rs[1, down, rows, :].astype(f32)
            gp[c, rows, :] = (total * slope[rows, :]).astype(bf16)

        def edge(rows):
            total = hid[c, rows, :].astype(f32) + rs[front, last - 1, rows, :].astype(f32)
            gp[c, rows, :] = (total * slope[rows, :]).astype(bf16)

        @pl.when(position(back) > 0)
        def _():
            strips(j * fine, fine, middle)

        @pl.when(position(back) == 0)
        def _():
            strips(j * fine, fine, edge)

        for side in (front, back):
            @pl.when(position(side) < last)
            def _():
                gp_copy(side, c, j, gp.at[c, piece(j)]).start()

        @pl.when(lax.rem(j, per) == per - 1)
        def _():
            use_rows(c, j // per)

    loop(0, F, own)

    @pl.when(position(back) == 0)
    def _():
        send_own(back, lead, F - 1)
        send_own_last(back)

    dy_far[...] = dy[pl.ds(q * far, q)].reshape(Tc, Dc)
    row_rest(x_ref, x, x_s, x_r)
    local[4].wait()

    tile_g = H // F

    def gs_tile(i):
        rows = pl.ds(pl.multiple_of(i * tile_g, tile_g), tile_g)
        left = act[pl.ds(back, last), :, rows].reshape(last * Tc, tile_g)
        right = dy[pl.ds(q * back, q * last)].reshape(last * Tc, Dc)
        gs[rows, :] = contract_first(left, right)

    def gf_tile(i):
        cols = pl.ds(pl.multiple_of(i * tile_g, tile_g), tile_g)
        right = gp[:, :, cols].reshape(N * Tc, tile_g)
        gf[:, cols] = contract_first(x[...].reshape(N * Tc, Dc), right) * factor

    def late_rounds(i):
        def body(side, j):
            p = position(side)

            @pl.when(p > i - N)
            def _():
                s = shard_at(side, p - 1 + N - i)
                gp_copy(side, s, j).wait_recv()

                @pl.when(p < last)
                def _():
                    gp_copy(side, s, j).start()

                gp_load(side, s, j).start()

                @pl.when(lax.rem(j, per) == per - 1)
                def _():
                    loop(j - per + 1, j + 1, lambda k: gp_load(side, s, k).wait())
                    use_rows(s, j // per)

            @pl.when((p == i - N) & (p >= 1) & (j >= early))
            def _():
                pre_move(side, 0, j)

        step = both(body)

        def one(jj):
            step(jj)

            @pl.when((i == 2 * N - 2) & (jj < F))
            def _():
                gs_tile(jj)

        loop(0, F + skew, one)

        def use(u):
            side = front + u * (back - front)
            p = position(side)

            @pl.when((p == i - N) & (p >= 1))
            def _():
                loop(early, F, lambda j: pre_use(side, 0, j))

        loop(0, 2, use)

    loop(N, 2 * N - 1, late_rounds)

    def finish():
        for k in range(1, R):
            p = lax.rem(r + k, R)
            row_got(gi_send.at[0, pl.ds(0, Tr)], gi_recv, p, gi_s.at[p], gi_r).wait_recv()

        def total_strip(rows):
            total = gi_recv[0, rows, :].astype(f32)
            for p in range(1, R):
                total = total + gi_recv[p, rows, :].astype(f32)
            gi[rows, :] = total.astype(bf16)

        strips(0, Tr, total_strip)

    def sent():
        dy_end()
        row_end(1, x_ref, x, x_s, x_r)
        for s in range(N):
            for i in range(q):
                @pl.when(q * s + i != r)
                def _():
                    gi_copy(s, i).wait_send()
        for side in (0, 1):
            p = position(side)
            for t in range(last):
                s = shard_at(side, t)

                @pl.when((p >= t) & (p < last))
                def _():
                    along(pre_in.at[s], pre_in.at[s], side, pr_s.at[side, s], pr_r.at[s, 0]).wait_send()
                    along(gp_in.at[s], gp_in.at[s], side, gp_s.at[side, s], gp_r.at[s, 0]).wait_send()

            for t in range(1, N):
                s = shard_at(side, t)

                @pl.when(p < t)
                def _():
                    along(hid.at[s], rs.at[side, t - 1], side, rs_s.at[side, t - 1],
                          rs_r.at[side, t - 1, 0]).wait_send()

    def last_round(j):
        @pl.when((position(front) == last) & (j < F - 1))
        def _():
            pre_move(front, 0, j)

        gf_tile(j)

        @pl.when((position(front) == last) & (j < F - 1))
        def _():
            pre_use(front, 0, j)

    loop(0, F, last_round)
    finish()
    sent()

    @pl.when(position(front) == last)
    def _():
        pre_move(front, 0, F - 1)


def exchange(R, N, factor, x, dy, pre, w1, w2):
    Tr, Dc = dy.shape
    Tc, H = pre.shape
    bf16, f32 = jnp.bfloat16, jnp.float32
    dma = pltpu.SemaphoreType.DMA
    F = 4
    hbm = pl.BlockSpec(memory_space=pltpu.HBM)
    vmem = pl.BlockSpec(memory_space=pltpu.VMEM)
    return pl.pallas_call(
        functools.partial(kernel, R, N, F, 2, 1, 1, 1, factor),
        out_shape=[
            pltpu.VMEM((Tr, Dc), bf16),
            pltpu.VMEM((H, Dc), f32),
            pltpu.VMEM((Dc, H), f32),
            pltpu.VMEM((N, Tc, H), bf16),
            pltpu.VMEM((Tc, Dc), bf16),
            pltpu.VMEM((N, Tc // F, H), bf16),
            jax.ShapeDtypeStruct((N, Tc, H), bf16),
            jax.ShapeDtypeStruct((N, Tc, H), bf16),
        ],
        in_specs=[hbm] * 5,
        out_specs=[vmem] * 6 + [hbm] * 2,
        scratch_shapes=[
            pltpu.VMEM(w1.shape, bf16),
            pltpu.VMEM(w2.shape, bf16),
            pltpu.VMEM((R, Tr, Dc), bf16),
            pltpu.VMEM((R, Tr, Dc), bf16),
            pltpu.VMEM((N, Tc, H), bf16),
            pltpu.VMEM((N, Tc, H), bf16),
            pltpu.VMEM((N, Tc, H), bf16),
            pltpu.VMEM((Tc, H), f32),
            pltpu.VMEM((2, N - 1, Tc, H), bf16),
            pltpu.VMEM((N, Tc, Dc), bf16),
            pltpu.VMEM((R, Tr, Dc), bf16),
            dma((5,)),
            dma((R // 2,)), dma((R,)), dma((R // 2,)), dma((R,)), dma((2, R // 2)),
            dma((2, N)), dma((N, F)),
            dma((2, N - 1)), dma((2, N - 1, F)),
            dma((2, N)), dma((N, F)),
            dma((R,)), dma((R,)), dma((2, F)), dma((2, F)), dma((2,)), dma((2,)),
        ],
        compiler_params=pltpu.CompilerParams(
            collective_id=0, has_side_effects=True, vmem_limit_bytes=40 * 2**20
        ),
    )(x, dy, pre, w1, w2)[:6]


def write_out(N, factor, gi, gs, gf, act, dy_far, tail):
    H, Dc = gs.shape
    Tc, fine = act.shape[1], tail.shape[1]
    tile = min(256, H)
    slots = 8

    def body(gi_ref, gs_ref, gf_ref, act_ref, dy_ref, tail_ref, gi_out, gf_out, gs_out, held, end, sems, gs_sems):
        far = (1 - (2 * lax.axis_index("col")) // N) * (N - 1)
        whole = [
            pltpu.make_async_copy(gi_ref, gi_out, sems.at[0]),
            pltpu.make_async_copy(gf_ref, gf_out, sems.at[1]),
        ]
        for copy in whole:
            copy.start()

        def act_strip(rows):
            end[rows, :] = act_of(tail_ref[far, rows, :].astype(jnp.float32)).astype(jnp.bfloat16)

        strips(0, fine, act_strip)

        def copy_of(i):
            rows = pl.ds(i * tile, tile)
            return pltpu.make_async_copy(held.at[i % slots], gs_out.at[rows], gs_sems.at[i % slots])

        for i in range(H // tile):
            rows = pl.ds(i * tile, tile)
            if i >= slots:
                copy_of(i - slots).wait()
            term = contract_first(act_ref[far, 0 : Tc - fine, rows], dy_ref[0 : Tc - fine, :])
            term = term + contract_first(end[:, rows], dy_ref[Tc - fine :, :])
            held[i % slots] = (gs_ref[rows, :] + term) * factor
            copy_of(i).start()
        for i in range(max(0, H // tile - slots), H // tile):
            copy_of(i).wait()
        for copy in whole:
            copy.wait()

    vmem = pl.BlockSpec(memory_space=pltpu.VMEM)
    hbm = pl.BlockSpec(memory_space=pltpu.HBM)
    dma = pltpu.SemaphoreType.DMA
    return pl.pallas_call(
        body,
        in_specs=[vmem] * 6,
        out_specs=[hbm] * 3,
        out_shape=[jax.ShapeDtypeStruct(a.shape, a.dtype) for a in (gi, gf, gs)],
        scratch_shapes=[
            pltpu.VMEM((slots, tile, Dc), jnp.float32), pltpu.VMEM((fine, H), jnp.bfloat16), dma((2,)), dma((slots,)),
        ],
        compiler_params=pltpu.CompilerParams(vmem_limit_bytes=16 * 2**20),
    )(gi, gs, gf, act, dy_far, tail)


def on_device(R, N, inputs_act, out_grad, pre_act, w_first, w_second):
    total_tokens = pre_act.shape[0] * N
    factor = 1.0 / math.sqrt(total_tokens)
    parts = exchange(R, N, factor, inputs_act, out_grad, pre_act, w_first, w_second)
    return tuple(write_out(N, factor, *parts))


def solution(mesh):
    in_specs = (P("row", "col"), P("row", "col"), P("col", "row"), P("col", "row"), P("row", "col"))
    out_specs = (P("row", "col"), P("col", "row"), P("row", "col"))
    return jax.shard_map(
        functools.partial(on_device, mesh.shape["row"], mesh.shape["col"]),
        mesh=mesh, in_specs=in_specs, out_specs=out_specs, check_vma=False,
    )
```

```python
import functools
import math

import jax
import jax.numpy as jnp
from jax import lax
from jax.experimental import pallas as pl
from jax.experimental.pallas import tpu as pltpu
from jax.sharding import PartitionSpec as P

gelu_coef = 0.044715
inner_c = math.sqrt(2.0 / math.pi)
STRIP = 16
MESH = pl.DeviceIdType.MESH


def tanh_of(p):
    return jnp.tanh(inner_c * (p + gelu_coef * p * p * p))


def act_of(p):
    return 0.5 * p * (1.0 + tanh_of(p))


def slope_of(p):
    t = tanh_of(p)
    return 0.5 * (1.0 + t) + 0.5 * p * (1.0 - t * t) * inner_c * (1.0 + 3.0 * gelu_coef * p * p)


def contract_last(left, right):
    return lax.dot_general(
        left, right, (((1,), (1,)), ((), ())), preferred_element_type=jnp.float32
    )


def contract_first(left, right):
    return lax.dot_general(
        left, right, (((0,), (0,)), ((), ())), preferred_element_type=jnp.float32
    )


def strips(first, count, body):
    def one(i, carry):
        body(pl.ds(pl.multiple_of(first + i * STRIP, STRIP), STRIP))
        return carry

    lax.fori_loop(0, count // STRIP, one, 0)


def kernel(
    R, N, F, lead, head, early, skew, factor,
    x_ref, dy_ref, pre_ref, w1_ref, w2_ref,
    gi, gs, gf, act, dy_far, tail, pre_in, gp_in,
    w1, w2, dy, x, hid, pre, gp, slope, rs, gi_send, gi_recv,
    loc, dy_s, dy_r, x_s, x_r, fw_s, pr_s, pr_r, rs_s, rs_r, gp_s, gp_r, gi_s, gi_r, pre_l, gp_l, rl_s, rl_r,
):
    r = lax.axis_index("row")
    c = lax.axis_index("col")
    q = R // N
    Tr = dy_ref.shape[0]
    Tc, H = pre_ref.shape
    Dc = dy_ref.shape[1]
    fine = Tc // F
    per = F // q
    last = N - 1
    f32, bf16 = jnp.float32, jnp.bfloat16

    sibling = r + 1 - 2 * lax.rem(r, 2)
    chips = R // 2
    square = chips == 4
    beside = r + 2 - 4 * lax.rem(r // 2, 2)
    across = lax.rem(r + 4, R)
    corner = lax.rem(beside + 4, R)

    barrier = pltpu.get_barrier_semaphore()
    greeted = [sibling, beside, across] if square else [lax.rem(r + k, R) for k in range(1, R)]
    for peer in greeted:
        pl.semaphore_signal(barrier, inc=1, device_id={"row": peer}, device_id_type=MESH)

    @pl.when(c > 0)
    def _():
        pl.semaphore_signal(barrier, inc=1, device_id={"col": c - 1}, device_id_type=MESH)

    @pl.when(c < last)
    def _():
        pl.semaphore_signal(barrier, inc=1, device_id={"col": c + 1}, device_id_type=MESH)

    local = [
        pltpu.make_async_copy(dy_ref, dy.at[r], loc.at[0]),
        pltpu.make_async_copy(pre_ref, pre.at[c], loc.at[1]),
        pltpu.make_async_copy(w2_ref, w2, loc.at[2]),
        pltpu.make_async_copy(w1_ref, w1, loc.at[3]),
        pltpu.make_async_copy(x_ref, x.at[r], loc.at[4]),
    ]
    for copy in local:
        copy.start()
    ends = jnp.where(c > 0, 1, 0) + jnp.where(c < last, 1, 0)
    pl.semaphore_wait(barrier, len(greeted) + ends)

    front = 1 - (2 * c) // N
    back = 1 - front
    far = front * last

    def position(side):
        return c + side * (last - 2 * c)

    def shard_at(side, t):
        return t + side * (last - 2 * t)

    def after(side):
        return c + 1 - 2 * side

    def loop(first, end, body):
        def one(i, carry):
            body(i)
            return carry

        lax.fori_loop(first, end, one, 0)

    def piece(j):
        return pl.ds(pl.multiple_of(j * fine, fine), fine)

    def row_send(src, dst, k, send, recv):
        to = sibling if k == 0 else lax.rem(r + 2 * k, R)
        return pltpu.make_async_remote_copy(
            src_ref=src, dst_ref=dst.at[r], send_sem=send.at[k], recv_sem=recv.at[r],
            device_id={"row": to}, device_id_type=MESH)

    def row_got(src, dst, p, send, recv):
        return pltpu.make_async_remote_copy(
            src_ref=src, dst_ref=dst.at[p], send_sem=send, recv_sem=recv.at[p],
            device_id={"row": sibling}, device_id_type=MESH)

    def row_forward(which, dst, k, recv):
        p = lax.rem(r + 2 * k, R)
        return pltpu.make_async_remote_copy(
            src_ref=dst.at[p], dst_ref=dst.at[p], send_sem=fw_s.at[which, k], recv_sem=recv.at[p],
            device_id={"row": sibling}, device_id_type=MESH)

    def row_start(src, dst, send, recv):
        for k in list(range(1, chips)) + [0]:
            row_send(src, dst, k, send, recv).start()

    def row_pass(which, src, dst, send, recv):
        for k in range(1, chips):
            row_got(src, dst, lax.rem(r + 2 * k, R), send.at[k], recv).wait_recv()
            row_forward(which, dst, k, recv).start()

    def row_rest(src, dst, send, recv):
        for k in range(chips):
            row_got(src, dst, lax.rem(sibling + 2 * k, R), send.at[k], recv).wait_recv()

    def row_end(which, src, dst, send, recv):
        for k in range(chips):
            row_send(src, dst, k, send, recv).wait_send()
            if k > 0:
                row_forward(which, dst, k, recv).wait_send()

    half = Tr // 2

    def to_row(src, dst, to, send, recv):
        return pltpu.make_async_remote_copy(
            src_ref=src, dst_ref=dst, send_sem=send, recv_sem=recv, device_id={"row": to}, device_id_type=MESH)

    def dy_own(slot):
        return to_row(dy_ref, dy.at[r], (sibling, beside, across)[slot], dy_s.at[slot], dy_r.at[r])

    def dy_share(slot):
        p = (beside, across, corner)[slot]
        return to_row(dy.at[p], dy.at[p], sibling, fw_s.at[0, slot], dy_r.at[p])

    def dy_got(p):
        to_row(dy_ref, dy.at[p], sibling, dy_s.at[0], dy_r.at[p]).wait_recv()

    def dy_relay(slot):
        place = dy.at[(beside, across)[slot], pl.ds(slot * half, half)]
        return to_row(place, place, (across, beside)[slot], rl_s.at[slot], rl_r.at[slot])

    def dy_corner(slot):
        place = dy.at[corner, pl.ds(slot * half, half)]
        to_row(place, place, sibling, rl_s.at[slot], rl_r.at[slot]).wait_recv()

    def dy_start():
        if not square:
            row_start(dy_ref, dy, dy_s, dy_r)
            return
        for slot in (1, 2, 0):
            dy_own(slot).start()

    def dy_gather():
        if not square:
            row_pass(0, dy_ref, dy, dy_s, dy_r)
            row_rest(dy_ref, dy, dy_s, dy_r)
            return
        for slot in range(2):
            dy_got((beside, across)[slot])
            dy_relay(slot).start()
            dy_share(slot).start()
        for slot in range(2):
            dy_corner(slot)
        dy_share(2).start()
        for k in range(chips):
            dy_got(lax.rem(sibling + 2 * k, R))

    def dy_end():
        if not square:
            row_end(0, dy_ref, dy, dy_s, dy_r)
            return
        for slot in range(3):
            dy_own(slot).wait_send()
            dy_share(slot).wait_send()
        for slot in range(2):
            dy_relay(slot).wait_send()

    def along(src, dst, side, send, recv):
        return pltpu.make_async_remote_copy(
            src_ref=src, dst_ref=dst, send_sem=send, recv_sem=recv,
            device_id={"col": after(side)}, device_id_type=MESH)

    def pre_copy(side, s, j, src=None):
        place = pre_in.at[s, piece(j)]
        return along(place if src is None else src, place, side, pr_s.at[side, s], pr_r.at[s, j])

    def pre_last(side, s, src=None):
        place = tail.at[s]
        return along(place if src is None else src, place, side, pr_s.at[side, s], pr_r.at[s, F - 1])

    def pre_load(side, s, j):
        return pltpu.make_async_copy(pre_in.at[s, piece(j)], pre.at[s, piece(j)], pre_l.at[side, j])

    def gp_copy(side, s, j, src=None):
        place = gp_in.at[s, piece(j)]
        return along(place if src is None else src, place, side, gp_s.at[side, s], gp_r.at[s, j])

    def gp_load(side, s, j):
        return pltpu.make_async_copy(gp_in.at[s, piece(j)], gp.at[s, piece(j)], gp_l.at[side, j])

    def rs_copy(side, t, j):
        return along(hid.at[shard_at(side, t), piece(j)], rs.at[side, t - 1, piece(j)], side,
                     rs_s.at[side, t - 1], rs_r.at[side, t - 1, j])

    def send_own(side, first, end):
        loop(first, end, lambda j: pre_copy(side, c, j, pre_ref.at[piece(j)]).start())

    def send_own_last(side):
        pre_last(side, c, pre_ref.at[piece(F - 1)]).start()

    for side in (front, back):
        @pl.when((position(side) < last) & (position(side) > 0))
        def _():
            send_own(side, 0, F - 1)
            send_own_last(side)

        @pl.when(position(side) == 0)
        def _():
            send_own(side, 0, lead)
    dy_start()

    local[1].wait()

    def slope_strip(rows):
        slope[rows, :] = slope_of(pre[c, rows, :].astype(f32))

    def act_rows(s, first, count):
        def one(rows):
            act[s, rows, :] = act_of(pre[s, rows, :].astype(f32)).astype(bf16)

        strips(first, count, one)

    strips(0, Tc, slope_strip)
    act_rows(c, 0, Tc)

    def pre_move(side, t, j):
        s = shard_at(side, t)

        @pl.when(j < F - 1)
        def _():
            pre_copy(side, s, j).wait_recv()

            @pl.when(position(side) < last)
            def _():
                pre_copy(side, s, j).start()

            pre_load(side, s, j).start()

        @pl.when(j == F - 1)
        def _():
            pre_last(side, s).wait_recv()

            @pl.when(position(side) < last)
            def _():
                pre_last(side, s).start()

    def pre_use(side, t, j):
        s = shard_at(side, t)

        @pl.when(j < F - 1)
        def _():
            pre_load(side, s, j).wait()
            act_rows(s, j * fine, fine)

        @pl.when((j == F - 1) & (s != far))
        def _():
            def one(i):
                rows = pl.ds(pl.multiple_of(i * STRIP, STRIP), STRIP)
                act[s, pl.ds(pl.multiple_of((F - 1) * fine + i * STRIP, STRIP), STRIP), :] = act_of(
                    tail[s, rows, :].astype(f32)).astype(bf16)

            loop(0, fine // STRIP, one)

    def next_pre(first, end):
        @pl.when(position(front) > 1)
        def _():
            loop(first, end, lambda j: pre_move(front, position(front) - 1, j))

        @pl.when(position(back) > 1)
        def _():
            loop(first, end, lambda j: pre_move(back, position(back) - 1, j))

    next_pre(0, head)

    local[0].wait()
    local[2].wait()
    dy_gather()
    row_start(x_ref, x, x_s, x_r)

    tile_h = min(512, H)

    def partial(k):
        t = last - k
        s = shard_at(back, t)

        def one(i):
            cols = pl.ds(pl.multiple_of(i * tile_h, tile_h), tile_h)
            left = dy[pl.ds(q * s, q)].reshape(Tc, Dc)
            hid[s, :, cols] = contract_last(left, w2[cols, :]).astype(bf16)

        loop(0, H // tile_h, one)

        @pl.when((position(back) == 0) & (t > 0))
        def _():
            loop(0, F, lambda j: rs_copy(back, t, j).start())

        next_pre(jnp.minimum(head + k, F), jnp.minimum(head + k + 1, F))

    loop(0, N, partial)

    def both(body):
        def one(jj):
            def turn(u):
                j = jj - u * skew

                @pl.when((j >= 0) & (j < F))
                def _():
                    body(front + u * (back - front), j)

            loop(0, 2, turn)

        return one

    def early_pre(side):
        loop(0, early, lambda j: pre_move(side, 0, j))
        loop(0, early, lambda j: pre_use(side, 0, j))

    def first_rounds(i):
        for side in (front, back):
            p = position(side)

            @pl.when(((i == max(N - 3, 1)) & (p == 1)) | ((i == N - 2) & (p >= 2) & (p < last)))
            def _():
                early_pre(side)

        def body(side, j):
            p = position(side)

            @pl.when((p > i) & ((i > 1) | (j >= head + N)))
            def _():
                pre_move(side, p - i, j)

            @pl.when((p >= 1) & (p <= i))
            def _():
                t = last - i + p
                s = shard_at(side, t)
                rs_copy(side, t, j).wait_recv()

                def add(rows):
                    total = hid[s, rows, :].astype(f32) + rs[side, t - 1, rows, :].astype(f32)
                    hid[s, rows, :] = total.astype(bf16)

                strips(j * fine, fine, add)
                rs_copy(side, t, j).start()

        loop(0, F + skew, both(body))

        def use(u):
            side = front + u * (back - front)
            p = position(side)

            @pl.when(p > i)
            def _():
                loop(0, F, lambda j: pre_use(side, p - i, j))

        loop(0, 2, use)

    loop(1, N - 1, first_rounds)
    row_pass(1, x_ref, x, x_s, x_r)
    local[3].wait()
    tile_d = min(512, Dc)

    def gi_copy(s, i):
        to = q * s + i
        return pltpu.make_async_remote_copy(
            src_ref=gi_send.at[s, pl.ds(i * Tr, Tr)], dst_ref=gi_recv.at[r],
            send_sem=gi_s.at[to], recv_sem=gi_r.at[r], device_id={"row": to}, device_id_type=MESH)

    def use_rows(s, i):
        rows = pl.ds(pl.multiple_of(i * Tr, Tr), Tr)

        def one(t):
            cols = pl.ds(pl.multiple_of(t * tile_d, tile_d), tile_d)
            gi_send[s, rows, cols] = contract_last(gp[s, rows, :], w1[cols, :]).astype(bf16)

        loop(0, Dc // tile_d, one)
        to = q * s + i

        @pl.when(to != r)
        def _():
            gi_copy(s, i).start()

        @pl.when(to == r)
        def _():
            gi_recv[r] = gi_send[s, rows, :]

    def own(j):
        for side in (front, back):
            @pl.when(position(side) > 0)
            def _():
                rs_copy(side, position(side), j).wait_recv()

        up = jnp.maximum(c - 1, 0)
        down = jnp.maximum(last - c - 1, 0)

        def middle(rows):
            total = hid[c, rows, :].astype(f32) + rs[0, up, rows, :].astype(f32)
            total = total + rs[1, down, rows, :].astype(f32)
            gp[c, rows, :] = (total * slope[rows, :]).astype(bf16)

        def edge(rows):
            total = hid[c, rows, :].astype(f32) + rs[front, last - 1, rows, :].astype(f32)
            gp[c, rows, :] = (total * slope[rows, :]).astype(bf16)

        @pl.when(position(back) > 0)
        def _():
            strips(j * fine, fine, middle)

        @pl.when(position(back) == 0)
        def _():
            strips(j * fine, fine, edge)

        for side in (front, back):
            @pl.when(position(side) < last)
            def _():
                gp_copy(side, c, j, gp.at[c, piece(j)]).start()

        @pl.when(lax.rem(j, per) == per - 1)
        def _():
            use_rows(c, j // per)

    loop(0, F, own)

    @pl.when(position(back) == 0)
    def _():
        send_own(back, lead, F - 1)
        send_own_last(back)

    dy_far[...] = dy[pl.ds(q * far, q)].reshape(Tc, Dc)
    row_rest(x_ref, x, x_s, x_r)
    local[4].wait()

    tile_g = H // F

    def gs_tile(i):
        rows = pl.ds(pl.multiple_of(i * tile_g, tile_g), tile_g)
        left = act[pl.ds(back, last), :, rows].reshape(last * Tc, tile_g)
        right = dy[pl.ds(q * back, q * last)].reshape(last * Tc, Dc)
        gs[rows, :] = contract_first(left, right)

    def gf_tile(i):
        cols = pl.ds(pl.multiple_of(i * tile_g, tile_g), tile_g)
        right = gp[:, :, cols].reshape(N * Tc, tile_g)
        gf[:, cols] = contract_first(x[...].reshape(N * Tc, Dc), right) * factor

    def late_rounds(i):
        def body(side, j):
            p = position(side)

            @pl.when(p > i - N)
            def _():
                s = shard_at(side, p - 1 + N - i)
                gp_copy(side, s, j).wait_recv()

                @pl.when(p < last)
                def _():
                    gp_copy(side, s, j).start()

                gp_load(side, s, j).start()

                @pl.when(lax.rem(j, per) == per - 1)
                def _():
                    loop(j - per + 1, j + 1, lambda k: gp_load(side, s, k).wait())
                    use_rows(s, j // per)

            @pl.when((p == i - N) & (p >= 1) & (j >= early))
            def _():
                pre_move(side, 0, j)

        step = both(body)

        def one(jj):
            step(jj)

            @pl.when((i == 2 * N - 2) & (jj < F))
            def _():
                gs_tile(jj)

        loop(0, F + skew, one)

        def use(u):
            side = front + u * (back - front)
            p = position(side)

            @pl.when((p == i - N) & (p >= 1))
            def _():
                loop(early, F, lambda j: pre_use(side, 0, j))

        loop(0, 2, use)

    loop(N, 2 * N - 1, late_rounds)

    def finish():
        for k in range(1, R):
            p = lax.rem(r + k, R)
            row_got(gi_send.at[0, pl.ds(0, Tr)], gi_recv, p, gi_s.at[p], gi_r).wait_recv()

        def total_strip(rows):
            total = gi_recv[0, rows, :].astype(f32)
            for p in range(1, R):
                total = total + gi_recv[p, rows, :].astype(f32)
            gi[rows, :] = total.astype(bf16)

        strips(0, Tr, total_strip)

    def sent():
        dy_end()
        row_end(1, x_ref, x, x_s, x_r)
        for s in range(N):
            for i in range(q):
                @pl.when(q * s + i != r)
                def _():
                    gi_copy(s, i).wait_send()
        for side in (0, 1):
            p = position(side)
            for t in range(last):
                s = shard_at(side, t)

                @pl.when((p >= t) & (p < last))
                def _():
                    along(pre_in.at[s], pre_in.at[s], side, pr_s.at[side, s], pr_r.at[s, 0]).wait_send()
                    along(gp_in.at[s], gp_in.at[s], side, gp_s.at[side, s], gp_r.at[s, 0]).wait_send()

            for t in range(1, N):
                s = shard_at(side, t)

                @pl.when(p < t)
                def _():
                    along(hid.at[s], rs.at[side, t - 1], side, rs_s.at[side, t - 1],
                          rs_r.at[side, t - 1, 0]).wait_send()

    def last_round(j):
        @pl.when((position(front) == last) & (j < F - 1))
        def _():
            pre_move(front, 0, j)

        gf_tile(j)

        @pl.when((position(front) == last) & (j < F - 1))
        def _():
            pre_use(front, 0, j)

    loop(0, F, last_round)
    finish()
    sent()

    @pl.when(position(front) == last)
    def _():
        pre_move(front, 0, F - 1)


def exchange(R, N, factor, x, dy, pre, w1, w2):
    Tr, Dc = dy.shape
    Tc, H = pre.shape
    bf16, f32 = jnp.bfloat16, jnp.float32
    dma = pltpu.SemaphoreType.DMA
    F = 4
    hbm = pl.BlockSpec(memory_space=pltpu.HBM)
    vmem = pl.BlockSpec(memory_space=pltpu.VMEM)
    return pl.pallas_call(
        functools.partial(kernel, R, N, F, 2, 0, 1, 1, factor),
        out_shape=[
            pltpu.VMEM((Tr, Dc), bf16),
            pltpu.VMEM((H, Dc), f32),
            pltpu.VMEM((Dc, H), f32),
            pltpu.VMEM((N, Tc, H), bf16),
            pltpu.VMEM((Tc, Dc), bf16),
            pltpu.VMEM((N, Tc // F, H), bf16),
            jax.ShapeDtypeStruct((N, Tc, H), bf16),
            jax.ShapeDtypeStruct((N, Tc, H), bf16),
        ],
        in_specs=[hbm] * 5,
        out_specs=[vmem] * 6 + [hbm] * 2,
        scratch_shapes=[
            pltpu.VMEM(w1.shape, bf16),
            pltpu.VMEM(w2.shape, bf16),
            pltpu.VMEM((R, Tr, Dc), bf16),
            pltpu.VMEM((R, Tr, Dc), bf16),
            pltpu.VMEM((N, Tc, H), bf16),
            pltpu.VMEM((N, Tc, H), bf16),
            pltpu.VMEM((N, Tc, H), bf16),
            pltpu.VMEM((Tc, H), f32),
            pltpu.VMEM((2, N - 1, Tc, H), bf16),
            pltpu.VMEM((N, Tc, Dc), bf16),
            pltpu.VMEM((R, Tr, Dc), bf16),
            dma((5,)),
            dma((R // 2,)), dma((R,)), dma((R // 2,)), dma((R,)), dma((2, R // 2)),
            dma((2, N)), dma((N, F)),
            dma((2, N - 1)), dma((2, N - 1, F)),
            dma((2, N)), dma((N, F)),
            dma((R,)), dma((R,)), dma((2, F)), dma((2, F)), dma((2,)), dma((2,)),
        ],
        compiler_params=pltpu.CompilerParams(
            collective_id=0, has_side_effects=True, vmem_limit_bytes=40 * 2**20
        ),
    )(x, dy, pre, w1, w2)[:6]


def write_out(N, factor, gi, gs, gf, act, dy_far, tail):
    H, Dc = gs.shape
    Tc, fine = act.shape[1], tail.shape[1]
    tile = min(256, H)
    slots = 8

    def body(gi_ref, gs_ref, gf_ref, act_ref, dy_ref, tail_ref, gi_out, gf_out, gs_out, held, end, sems, gs_sems):
        far = (1 - (2 * lax.axis_index("col")) // N) * (N - 1)
        whole = [
            pltpu.make_async_copy(gi_ref, gi_out, sems.at[0]),
            pltpu.make_async_copy(gf_ref, gf_out, sems.at[1]),
        ]
        for copy in whole:
            copy.start()

        def act_strip(rows):
            end[rows, :] = act_of(tail_ref[far, rows, :].astype(jnp.float32)).astype(jnp.bfloat16)

        strips(0, fine, act_strip)

        def copy_of(i):
            rows = pl.ds(i * tile, tile)
            return pltpu.make_async_copy(held.at[i % slots], gs_out.at[rows], gs_sems.at[i % slots])

        for i in range(H // tile):
            rows = pl.ds(i * tile, tile)
            if i >= slots:
                copy_of(i - slots).wait()
            term = contract_first(act_ref[far, 0 : Tc - fine, rows], dy_ref[0 : Tc - fine, :])
            term = term + contract_first(end[:, rows], dy_ref[Tc - fine :, :])
            held[i % slots] = (gs_ref[rows, :] + term) * factor
            copy_of(i).start()
        for i in range(max(0, H // tile - slots), H // tile):
            copy_of(i).wait()
        for copy in whole:
            copy.wait()

    vmem = pl.BlockSpec(memory_space=pltpu.VMEM)
    hbm = pl.BlockSpec(memory_space=pltpu.HBM)
    dma = pltpu.SemaphoreType.DMA
    return pl.pallas_call(
        body,
        in_specs=[vmem] * 6,
        out_specs=[hbm] * 3,
        out_shape=[jax.ShapeDtypeStruct(a.shape, a.dtype) for a in (gi, gf, gs)],
        scratch_shapes=[
            pltpu.VMEM((slots, tile, Dc), jnp.float32), pltpu.VMEM((fine, H), jnp.bfloat16), dma((2,)), dma((slots,)),
        ],
        compiler_params=pltpu.CompilerParams(vmem_limit_bytes=16 * 2**20),
    )(gi, gs, gf, act, dy_far, tail)


def on_device(R, N, inputs_act, out_grad, pre_act, w_first, w_second):
    total_tokens = pre_act.shape[0] * N
    factor = 1.0 / math.sqrt(total_tokens)
    parts = exchange(R, N, factor, inputs_act, out_grad, pre_act, w_first, w_second)
    return tuple(write_out(N, factor, *parts))


def solution(mesh):
    in_specs = (P("row", "col"), P("row", "col"), P("col", "row"), P("col", "row"), P("row", "col"))
    out_specs = (P("row", "col"), P("col", "row"), P("row", "col"))
    return jax.shard_map(
        functools.partial(on_device, mesh.shape["row"], mesh.shape["col"]),
        mesh=mesh, in_specs=in_specs, out_specs=out_specs, check_vma=False,
    )
```
